512 devices in a mesh: pw: 8 (over x, y_hi), band: 64 (over y_lo, z, core).
Axes of the slice: x: 4, y: 4 (y_hi: 2, y_lo: 2; y = y_hi * 2 + y_lo), z: 16, core: 2. Of those that a mesh axis runs over, the one named last changes fastest.
Arguments:
- stick_coefs: float32 [64, 8, 48, 1024], P('band', None, None, 'pw'), may hold values from -6 to 6
- miller: int32 [2, 1024], P(None, 'pw'), may hold values from 0 to 47, as said below
- stick_count: int32 [8], P('pw'), may hold values from 1 to 128, as said below
Outputs:
- exchange_coefs: float32 [64, 8, 48, 1024], P('band', None, None, 'pw')
The draws below stay inside these ranges and needn't reach their ends.
Inputs may be any that keep to these rules, and one draw needn't show every extreme that they name: `stick_count`: some pw index has exactly 128 live sticks. Over the live slots the columns (miller[0, s], miller[1, s]) are distinct and are the columns of smallest sigma(miller[0])**2 + sigma(miller[1])**2, as many as there are live slots (ties at the edge broken arbitrarily); the other slots hold arbitrary columns.
All inputs are finite; a program needn't handle non-finite values.
Results may differ from the reference program's by a relative error of at most 0.0003.
Values sent between devices are 32-bit elements; how exact they have to be, the bound alone decides.
A program may use at most 64 MiB of HBM per device.

```python
import math
import jax
import jax.numpy as jnp
from jax import lax

NGRID = 48
STK_DEV = 128
ORB_DEV = 1
HALF = 2
NG = 64
NMEM = 8
STICKS = 1024


def stick_plan(key):
    subkeys = jax.random.split(jax.random.fold_in(key, 5183), 5)
    owners = STICKS // STK_DEV
    counts = jax.random.randint(subkeys[0], (owners,), STK_DEV // 8, STK_DEV + 1)
    fullest = jax.random.randint(subkeys[1], (), 0, owners)
    counts = jnp.where(jnp.arange(owners) == fullest, STK_DEV, counts).astype(jnp.int32)
    live_total = jnp.sum(counts)
    columns = NGRID * NGRID
    col_ids = jnp.arange(columns, dtype=jnp.int32)
    first_index = col_ids // NGRID
    second_index = col_ids % NGRID
    signed_first = jnp.where(first_index < NGRID // 2, first_index, first_index - NGRID)
    signed_second = jnp.where(second_index < NGRID // 2, second_index, second_index - NGRID)
    radius = signed_first * signed_first + signed_second * signed_second
    tiebreak = jax.random.permutation(subkeys[2], columns).astype(jnp.int32)
    by_radius = jnp.argsort(radius * columns + tiebreak, stable=True)
    shuffle = jax.random.permutation(subkeys[3], columns).astype(jnp.int32)
    position = jnp.arange(columns, dtype=jnp.int32)
    shuffle_score = jnp.where(position < live_total, shuffle, columns + position)
    picked = by_radius[jnp.argsort(shuffle_score, stable=True)]
    slot_ids = jnp.arange(STICKS, dtype=jnp.int32)
    slot_owner = slot_ids // STK_DEV
    slot_pos = slot_ids % STK_DEV
    offsets = jnp.cumsum(counts) - counts
    live_rank = jnp.minimum(offsets[slot_owner] + slot_pos, columns - 1)
    live_slot = slot_pos < counts[slot_owner]
    filler = jax.random.randint(subkeys[4], (STICKS,), 0, columns)
    column = jnp.where(live_slot, picked[live_rank], filler).astype(jnp.int32)
    miller = jnp.stack([column // NGRID, column % NGRID]).astype(jnp.int32)
    return (counts, miller)


def draw_miller(key, part):
    return stick_plan(key)[1]


def draw_stick_count(key, part):
    return stick_plan(key)[0]


def shard_levels(key, shape, pieces, least, top_value):
    level, own = 1.0, jax.random.fold_in(key, 6)
    for axis_at, parts in pieces:
        steps = jnp.exp(jax.random.uniform(jax.random.fold_in(own, axis_at), (parts,), jnp.float32, least / len(pieces), top_value / len(pieces)))
        level = level * jnp.repeat(steps, shape[axis_at] // parts).reshape([-1 if axis == axis_at else 1 for axis in range(len(shape))])
    return level


def normal_values(own_key, extent, scale, most, pieces=(), kind=jnp.bfloat16):
    drawn = jax.random.normal(own_key, extent, jnp.float32) * scale
    if len(pieces) > 0:
        drawn = shard_levels(own_key, extent, pieces, -0.22, 0.18) * drawn
    return jnp.clip(drawn, min=-most, max=most).astype(kind)


def setup_inputs(seed: int = 0) -> dict:
    arg_keys = jax.random.split(jax.random.key(seed), 4)
    return {
        "stick_coefs": normal_values(arg_keys[0], (NG, NMEM, NGRID, STICKS), 1.0, 6.0, ((0, 64), (3, 8)), jnp.float32),
        "miller": draw_miller(jax.random.fold_in(arg_keys[3], 71), 0),
        "stick_count": draw_stick_count(jax.random.fold_in(arg_keys[3], 71), 0),
    }


kernel_scale = 4.0
screen_width = 16.0

def hartley_axis(cube_field, axis_id):
    spectrum = jnp.fft.fft(cube_field, axis=axis_id)
    return jnp.real(spectrum) - jnp.imag(spectrum)

def hartley_cube(cube_field):
    for axis_id in (-3, -2, -1):
        cube_field = hartley_axis(cube_field, axis_id)
    return cube_field

def coulomb_kernel(points):
    indices = jnp.arange(points)
    signed = jnp.where(indices < points // 2, indices, indices - points).astype(jnp.float32)
    squares = signed * signed
    radius_sq = squares[:, None, None] + squares[None, :, None] + squares[None, None, :]
    scaled = radius_sq / screen_width
    divisor = jnp.where(radius_sq > 0, scaled, jnp.float32(1.0))
    return kernel_scale * jnp.where(radius_sq > 0, -jnp.expm1(-divisor) / divisor, jnp.float32(1.0))

def synthesize(group_coefs, miller, live_mask):
    points = group_coefs.shape[1]
    cube_grid = jnp.zeros((group_coefs.shape[0], points, points, points), jnp.float32)
    cube_grid = cube_grid.at[:, :, miller[0], miller[1]].add(group_coefs * live_mask)
    return hartley_cube(cube_grid) / math.sqrt(points ** 3)

def poisson(density, kernel):
    points = density.shape[-1]
    return hartley_cube(kernel * hartley_cube(density)) / float(points ** 3)

def reference(stick_coefs, miller, stick_count):
    groups = stick_coefs.shape[0]
    members = stick_coefs.shape[1]
    points = stick_coefs.shape[2]
    owners = stick_count.shape[0]
    per_owner = stick_coefs.shape[3] // owners
    position = jnp.arange(per_owner, dtype=jnp.int32)
    live_mask = (position[None, :] < stick_count[:, None]).reshape(-1).astype(jnp.float32)
    kernel = coulomb_kernel(points)

    def group_result(group):
        own_orbs = synthesize(stick_coefs[group], miller, live_mask)
        own_orbs = own_orbs.reshape(owners, ORB_DEV, points, points, points)
        exch_field = jnp.zeros_like(own_orbs)
        for offset in range(-HALF, HALF + 1):
            if offset == 0:
                visitor = own_orbs
            else:
                other = jnp.mod(group + offset, groups).astype(jnp.int32)
                visitor = synthesize(stick_coefs[other], miller, live_mask)
                visitor = visitor.reshape(owners, ORB_DEV, points, points, points)
            for left_idx in range(ORB_DEV):
                for right_idx in range(ORB_DEV):
                    potential = poisson(own_orbs[:, left_idx] * visitor[:, right_idx], kernel)
                    exch_field = exch_field.at[:, left_idx].add(-potential * visitor[:, right_idx])
        exch_field = exch_field.reshape(members, points, points, points)
        spectrum = hartley_cube(exch_field) / math.sqrt(points ** 3)
        return spectrum[:, :, miller[0], miller[1]] * live_mask
    return lax.map(group_result, jnp.arange(groups, dtype=jnp.int32))
```

```python
import math

import jax
import jax.numpy as jnp
import numpy as np
from jax import lax
from jax.experimental import pallas as pl
from jax.experimental.pallas import tpu as pltpu
from jax.sharding import PartitionSpec as P

N = 48
HALF = 2
PAIRS = 2 * HALF + 1
COLS = N * N
WIDE = 256
OWNERS = 8
STK = 128
STICKS = OWNERS * STK
F32, BF16, I32 = jnp.float32, jnp.bfloat16, jnp.int32
MESH = pl.DeviceIdType.MESH
SHIFTS = (-2, -1, 1, 2)


def split_table(values):
    high = np.asarray(values, np.float32).astype(jnp.bfloat16)
    rest = np.asarray(values, np.float64) - high.astype(np.float64)
    low = rest.astype(np.float32).astype(jnp.bfloat16)
    tail = (rest - low.astype(np.float64)).astype(np.float32).astype(jnp.bfloat16)
    return high, low, tail


def constant_tables():
    index = np.arange(N)
    angles = 2.0 * math.pi / N * ((index[:, None] * index[None, :]) % N)
    cas = np.cos(angles) + np.sin(angles)
    high, low, tail = split_table(cas)
    left = np.concatenate([high, high, low], axis=1)
    exact = np.concatenate([high, low, tail], axis=1)
    block = np.kron(np.eye(PAIRS), cas)
    block = np.pad(block, ((0, WIDE - PAIRS * N), (0, WIDE - PAIRS * N)))
    turn = split_table(block)[:2]
    enter = split_table(block * N**-1.5)[:2]
    leave = np.pad(np.tile(-cas * N**-1.5, (1, PAIRS)), ((0, 0), (0, WIDE - PAIRS * N)))
    leave = split_table(leave)[:2]
    repeat = np.zeros((WIDE, WIDE))
    repeat[:N, : PAIRS * N] = np.tile(np.eye(N), (1, PAIRS))
    repeat = repeat.astype(jnp.bfloat16)
    return [np.stack([left, exact]), np.stack(turn), np.stack(enter), np.stack(leave), repeat]


def split(value):
    high = value.astype(BF16)
    low = (value - high.astype(F32)).astype(BF16)
    return high, low


def dot(a, b):
    return lax.dot_general(a, b, (((1,), (0,)), ((), ())), preferred_element_type=F32)


def dot_nt(a, b):
    return lax.dot_general(a, b, (((1,), (1,)), ((), ())), preferred_element_type=F32)


def left3(table, value):
    high, low = split(value)
    return dot(table, jnp.concatenate([high, low, high], axis=0))


def right3(value, high_t, low_t):
    high, low = split(value)
    return dot(high, high_t) + dot(low, high_t) + dot(high, low_t)


def rows_of(y, count=1):
    return pl.ds(pl.multiple_of(y * (count * N), count * N), count * N)


def screened_kernel(kern):
    lanes = lax.broadcasted_iota(I32, (1, WIDE), 1)
    kx = lanes - N * (lanes // N)
    kx = jnp.where(kx < N // 2, kx, kx - N)
    rows = lax.broadcasted_iota(I32, (N, 1), 0)
    kz = jnp.where(rows < N // 2, rows, rows - N)
    flat_q = (kz * kz + kx * kx).astype(F32)

    def slab(y, carry):
        signed = jnp.where(y < N // 2, y, y - N)
        q = flat_q + (signed * signed).astype(F32)
        scaled = jnp.maximum(q, 1.0) * (1.0 / 16.0)
        value = (4.0 / N**3) * (1.0 - jnp.exp(-scaled)) / scaled
        kern[rows_of(y), :] = jnp.where(q > 0, value, 4.0 / N**3)
        return carry

    lax.fori_loop(0, N, slab, 0)


def stick_weights(tables, left_ref, cas_y, w_hi, w_lo):
    table = jnp.concatenate([tables[q] for q in range(OWNERS)], axis=1)
    iy, iz, live = table[0:1, :], table[1:2, :], table[2:3, :]
    grid_rows = lax.broadcasted_iota(I32, (N, STICKS), 0)
    pick_y = jnp.where(grid_rows == iy, 1.0, 0.0).astype(BF16)
    pick_z = jnp.where((grid_rows == iz) & (live > 0), 1.0, 0.0).astype(BF16)
    exact = left_ref[1]
    cas_y[...] = dot(exact, jnp.concatenate([pick_y] * 3, axis=0))
    cas_z = dot(exact, jnp.concatenate([pick_z] * 3, axis=0))

    def slab(y, carry):
        high, low = split(cas_y[pl.ds(y, 1), :] * cas_z)
        w_hi[rows_of(y), :] = high
        w_lo[rows_of(y), :] = low
        return carry

    lax.fori_loop(0, N, slab, 0)


def synthesize(slots, enter_ref, w_hi, w_lo, orb):
    enter_hi, enter_lo = enter_ref[0, :, 0 : PAIRS * N], enter_ref[1, :, 0 : PAIRS * N]
    highs, lows = [], []
    for q in range(OWNERS):
        coefs = jnp.concatenate([slots[d, q] for d in range(PAIRS)], axis=0)
        high, low = split(coefs)
        lines = dot(enter_hi, high) + dot(enter_hi, low) + dot(enter_lo, high)
        high, low = split(lines)
        highs.append(high)
        lows.append(low)
    line_hi, line_lo = jnp.concatenate(highs, axis=1), jnp.concatenate(lows, axis=1)
    step = 384
    for start in range(0, COLS, step):
        wh, wl = w_hi[start : start + step, :], w_lo[start : start + step, :]
        orb[start : start + step, :] = dot_nt(wh, line_hi) + dot_nt(wh, line_lo) + dot_nt(wl, line_hi)


def pair_fields(left_ref, turn_ref, repeat_ref, orb, work0, work1, kern):
    left = left_ref[0]
    turn_hi, turn_lo = turn_ref[0], turn_ref[1]
    repeat = repeat_ref[...]
    group = 4

    def forward(i, carry):
        value = orb[rows_of(i, group), :]
        high, low = split(value)
        density = (dot(high, repeat) + dot(low, repeat)) * value
        along_x = right3(density, turn_hi, turn_lo)
        for j in range(group):
            res = left3(left, along_x[j * N : (j + 1) * N])
            y = i * group + j
            work0[pl.ds(y, N, stride=N), :] = res[:, 0:128]
            work1[pl.ds(y, N, stride=N), :] = res[:, 128:256]
        return carry

    lax.fori_loop(0, N // group, forward, 0)

    def middle(i, carry):
        for j in range(group):
            at = rows_of(i * group + j)
            value = jnp.concatenate([work0[at, :], work1[at, :]], axis=1)
            res = left3(left, value) * kern[at, :]
            res = left3(left, res)
            work0[at, :] = res[:, 0:128]
            work1[at, :] = res[:, 128:256]
        return carry

    lax.fori_loop(0, N // group, middle, 0)

    def backward(i, carry):
        parts = []
        for j in range(group):
            at = pl.ds(i * group + j, N, stride=N)
            value = jnp.concatenate([work0[at, :], work1[at, :]], axis=1)
            parts.append(left3(left, value))
        value = jnp.concatenate(parts, axis=0)
        at = rows_of(i, group)
        orb[at, :] = right3(value, turn_hi, turn_lo) * orb[at, :]
        return carry

    lax.fori_loop(0, N // group, backward, 0)


def project(leave_ref, w_hi, w_lo, orb, result):
    leave_hi, leave_lo = leave_ref[0], leave_ref[1]
    total = jnp.zeros((N, STICKS), F32)
    step = 768
    for start in range(0, COLS, step):
        high, low = split(orb[start : start + step, :])
        field = dot_nt(leave_hi, high) + dot_nt(leave_hi, low) + dot_nt(leave_lo, high)
        high, low = split(field)
        wh, wl = w_hi[start : start + step, :], w_lo[start : start + step, :]
        pieces = dot(jnp.concatenate([high, low], axis=0), wh)
        total = total + pieces[0:N] + pieces[N : 2 * N] + dot(high, wl)
    for q in range(OWNERS):
        result[q] = total[:, q * STK : (q + 1) * STK]


def everything(
    coefs_ref, table_ref, left_ref, turn_ref, enter_ref, leave_ref, repeat_ref, out_ref,
    slots, tables, w_hi, w_lo, orb, work0, work1, kern, cas_y, result,
    table_send, table_recv, deal_send, slot_recv, pass_send, back_send, back_recv, local_sem,
):
    owner = lax.axis_index("pw")
    group = lax.axis_index("band")
    groups = lax.axis_size("band")
    barrier = pltpu.get_barrier_semaphore()
    for r in range(1, OWNERS):
        pl.semaphore_signal(barrier, inc=1, device_id={"pw": (owner + r) % OWNERS}, device_id_type=MESH)
    for shift in SHIFTS:
        pl.semaphore_signal(barrier, inc=1, device_id={"band": (group + shift + groups) % groups}, device_id_type=MESH)
    keep = pltpu.make_async_copy(coefs_ref.at[0, owner], slots.at[0, owner], local_sem.at[0])
    keep.start()
    keep_table = pltpu.make_async_copy(table_ref, tables.at[owner], local_sem.at[1])
    keep_table.start()
    pl.semaphore_wait(barrier, OWNERS - 1 + len(SHIFTS))

    started = []
    for r in range(1, OWNERS):
        target = (owner + r) % OWNERS
        send = pltpu.make_async_remote_copy(
            src_ref=table_ref, dst_ref=tables.at[owner],
            send_sem=table_send.at[r - 1], recv_sem=table_recv.at[r - 1],
            device_id={"pw": target}, device_id_type=MESH)
        send.start()
        started.append(send)
        send = pltpu.make_async_remote_copy(
            src_ref=coefs_ref.at[0, target], dst_ref=slots.at[0, owner],
            send_sem=deal_send.at[r - 1], recv_sem=slot_recv.at[0, r],
            device_id={"pw": target}, device_id_type=MESH)
        send.start()
        started.append(send)

    passed = []

    def pass_on(r):
        source = (owner + OWNERS - r) % OWNERS
        for at, shift in enumerate(SHIFTS):
            send = pltpu.make_async_remote_copy(
                src_ref=slots.at[0, source], dst_ref=slots.at[at + 1, source],
                send_sem=pass_send.at[at, r], recv_sem=slot_recv.at[at + 1, r],
                device_id={"band": (group + shift + groups) % groups}, device_id_type=MESH)
            send.start()
            passed.append(send)

    keep.wait()
    pass_on(0)
    for r in range(1, OWNERS):
        started[2 * r - 1].wait_recv()
        pass_on(r)
    keep_table.wait()
    for r in range(1, OWNERS):
        started[2 * r - 2].wait_recv()

    screened_kernel(kern)
    stick_weights(tables, left_ref, cas_y, w_hi, w_lo)
    for send in passed:
        send.wait_recv()
    synthesize(slots, enter_ref, w_hi, w_lo, orb)
    pair_fields(left_ref, turn_ref, repeat_ref, orb, work0, work1, kern)
    project(leave_ref, w_hi, w_lo, orb, result)

    keep = pltpu.make_async_copy(result.at[owner], out_ref.at[0, owner], local_sem.at[0])
    keep.start()
    back = []
    for r in range(1, OWNERS):
        target = (owner + r) % OWNERS
        send = pltpu.make_async_remote_copy(
            src_ref=result.at[target], dst_ref=out_ref.at[0, owner],
            send_sem=back_send.at[r - 1], recv_sem=back_recv.at[r - 1],
            device_id={"pw": target}, device_id_type=MESH)
        send.start()
        back.append(send)
    for send in started + passed:
        send.wait_send()
    keep.wait()
    for send in back:
        send.wait()


def shards(stick_coefs, miller, stick_count):
    position = jnp.arange(STK, dtype=I32)
    live = (position < stick_count[0]).astype(I32)
    table = jnp.concatenate([miller, live[None], jnp.zeros((5, STK), I32)], axis=0)
    vmem = pl.BlockSpec(memory_space=pltpu.VMEM)
    hbm = pl.BlockSpec(memory_space=pl.ANY)
    dma = pltpu.SemaphoreType.DMA
    return pl.pallas_call(
        everything,
        out_shape=jax.ShapeDtypeStruct((1, OWNERS, N, STK), F32),
        in_specs=[hbm] + [vmem] * 6,
        out_specs=hbm,
        scratch_shapes=[
            pltpu.VMEM((PAIRS, OWNERS, N, STK), F32),
            pltpu.VMEM((OWNERS, 8, STK), I32),
            pltpu.VMEM((COLS, STICKS), BF16),
            pltpu.VMEM((COLS, STICKS), BF16),
            pltpu.VMEM((COLS, WIDE), F32),
            pltpu.VMEM((COLS, 128), F32),
            pltpu.VMEM((COLS, 128), F32),
            pltpu.VMEM((COLS, WIDE), F32),
            pltpu.VMEM((N, STICKS), F32),
            pltpu.VMEM((OWNERS, N, STK), F32),
            dma((OWNERS - 1,)),
            dma((OWNERS - 1,)),
            dma((OWNERS - 1,)),
            dma((PAIRS, OWNERS)),
            dma((PAIRS - 1, OWNERS)),
            dma((OWNERS - 1,)),
            dma((OWNERS - 1,)),
            dma((2,)),
        ],
        compiler_params=pltpu.CompilerParams(
            vmem_limit_bytes=60 * 1024 * 1024, collective_id=0, has_side_effects=True
        ),
        name="exchange",
    )(stick_coefs, table, *[jnp.asarray(t) for t in constant_tables()])


def solution(mesh):
    return jax.shard_map(
        shards,
        mesh=mesh,
        in_specs=(P("band", None, None, "pw"), P(None, "pw"), P("pw")),
        out_specs=P("band", None, None, "pw"),
        check_vma=False,
    )
```

```python
import math

import jax
import jax.numpy as jnp
import numpy as np
from jax import lax
from jax.experimental import pallas as pl
from jax.experimental.pallas import tpu as pltpu
from jax.sharding import PartitionSpec as P

N = 48
HALF = 2
PAIRS = 2 * HALF + 1
COLS = N * N
WIDE = 256
OWNERS = 8
STK = 128
STICKS = OWNERS * STK
F32, BF16, I32 = jnp.float32, jnp.bfloat16, jnp.int32
MESH = pl.DeviceIdType.MESH
SHIFTS = (-2, -1, 1, 2)


def split_table(values):
    high = np.asarray(values, np.float32).astype(jnp.bfloat16)
    rest = np.asarray(values, np.float64) - high.astype(np.float64)
    low = rest.astype(np.float32).astype(jnp.bfloat16)
    tail = (rest - low.astype(np.float64)).astype(np.float32).astype(jnp.bfloat16)
    return high, low, tail


def constant_tables():
    index = np.arange(N)
    angles = 2.0 * math.pi / N * ((index[:, None] * index[None, :]) % N)
    cas = np.cos(angles) + np.sin(angles)
    high, low, tail = split_table(cas)
    left = np.concatenate([high, high, low], axis=1)
    exact = np.concatenate([high, low, tail], axis=1)
    block = np.kron(np.eye(PAIRS), cas)
    block = np.pad(block, ((0, WIDE - PAIRS * N), (0, WIDE - PAIRS * N)))
    turn = split_table(block)[:2]
    enter = split_table(block * N**-1.5)[:2]
    leave = np.pad(np.tile(-cas * N**-1.5, (1, PAIRS)), ((0, 0), (0, WIDE - PAIRS * N)))
    leave = split_table(leave)[:2]
    return [np.stack([left, exact]), np.stack(turn), np.stack(enter), np.stack(leave)]


def split(value):
    high = value.astype(BF16)
    low = (value - high.astype(F32)).astype(BF16)
    return high, low


def dot(a, b):
    return lax.dot_general(a, b, (((1,), (0,)), ((), ())), preferred_element_type=F32)


def dot_nt(a, b):
    return lax.dot_general(a, b, (((1,), (1,)), ((), ())), preferred_element_type=F32)


def left3(table, value):
    high, low = split(value)
    return dot(table, jnp.concatenate([high, low, high], axis=0))


def right3(value, high_t, low_t):
    high, low = split(value)
    return dot(high, high_t) + dot(low, high_t) + dot(high, low_t)


def rows_of(y, count=1):
    return pl.ds(pl.multiple_of(y * (count * N), count * N), count * N)


def screened_kernel(kern):
    lanes = lax.broadcasted_iota(I32, (1, WIDE), 1)
    kx = lanes - N * (lanes // N)
    kx = jnp.where(kx < N // 2, kx, kx - N)
    rows = lax.broadcasted_iota(I32, (N, 1), 0)
    kz = jnp.where(rows < N // 2, rows, rows - N)
    flat_q = (kz * kz + kx * kx).astype(F32)

    def slab(y, carry):
        signed = jnp.where(y < N // 2, y, y - N)
        q = flat_q + (signed * signed).astype(F32)
        scaled = jnp.maximum(q, 1.0) * (1.0 / 16.0)
        value = (4.0 / N**3) * (1.0 - jnp.exp(-scaled)) / scaled
        kern[rows_of(y), :] = jnp.where(q > 0, value, 4.0 / N**3)
        return carry

    lax.fori_loop(0, N, slab, 0)


def stick_weights(tables, left_ref, cas_y, w_hi, w_lo):
    table = jnp.concatenate([tables[q] for q in range(OWNERS)], axis=1)
    iy, iz, live = table[0:1, :], table[1:2, :], table[2:3, :]
    grid_rows = lax.broadcasted_iota(I32, (N, STICKS), 0)
    pick_y = jnp.where(grid_rows == iy, 1.0, 0.0).astype(BF16)
    pick_z = jnp.where((grid_rows == iz) & (live > 0), 1.0, 0.0).astype(BF16)
    exact = left_ref[1]
    cas_y[...] = dot(exact, jnp.concatenate([pick_y] * 3, axis=0))
    cas_z = dot(exact, jnp.concatenate([pick_z] * 3, axis=0))

    def slab(y, carry):
        high, low = split(cas_y[pl.ds(y, 1), :] * cas_z)
        w_hi[rows_of(y), :] = high
        w_lo[rows_of(y), :] = low
        return carry

    lax.fori_loop(0, N, slab, 0)


def synthesize(t, slots, enter_ref, w_hi, w_lo, orb):
    enter_hi, enter_lo = enter_ref[0, :, 0 : PAIRS * N], enter_ref[1, :, 0 : PAIRS * N]
    coefs = [jnp.concatenate([slots[d, r] for d in range(PAIRS)], axis=0) for r in (2 * t, 2 * t + 1)]
    high, low = split(jnp.concatenate(coefs, axis=1))
    lines = dot(enter_hi, high) + dot(enter_hi, low) + dot(enter_lo, high)
    line_hi, line_lo = split(lines)
    cols = slice(2 * t * STK, 2 * (t + 1) * STK)
    step = 384
    for start in range(0, COLS, step):
        at = slice(start, start + step)
        wh, wl = w_hi[at, cols], w_lo[at, cols]
        part = dot_nt(wh, line_hi) + dot_nt(wh, line_lo) + dot_nt(wl, line_hi)
        orb[at, :] = part if t == 0 else orb[at, :] + part


def spread_own(value):
    own = value[:, 0:128]
    lane = lax.broadcasted_iota(I32, own.shape, 1)
    by96 = pltpu.roll(own, 96, 1)
    first = jnp.where(lane < 48, own, jnp.where(lane < 96, pltpu.roll(own, 48, 1), by96))
    second = jnp.where(lane < 16, by96, jnp.where(lane < 64, pltpu.roll(own, 16, 1), pltpu.roll(own, 64, 1)))
    return jnp.concatenate([first, second], axis=1)


GROUPS = (24, 48, 24)


def pair_fields(left_ref, turn_ref, orb, work0, work1, kern):
    left = left_ref[0]
    turn_hi, turn_lo = turn_ref[0], turn_ref[1]
    group = GROUPS[0]

    def forward(i, carry):
        value = orb[rows_of(i, group), :]
        density = spread_own(value) * value
        along_x = right3(density, turn_hi, turn_lo)
        for j in range(group):
            res = left3(left, along_x[j * N : (j + 1) * N])
            y = i * group + j
            work0[pl.ds(y, N, stride=N), :] = res[:, 0:128]
            work1[pl.ds(y, N, stride=N), :] = res[:, 128:256]
        return carry

    lax.fori_loop(0, N // group, forward, 0)
    group_m = GROUPS[1]

    def middle(i, carry):
        for j in range(group_m):
            at = rows_of(i * group_m + j)
            value = jnp.concatenate([work0[at, :], work1[at, :]], axis=1)
            res = left3(left, value) * kern[at, :]
            res = left3(left, res)
            work0[at, :] = res[:, 0:128]
            work1[at, :] = res[:, 128:256]
        return carry

    lax.fori_loop(0, N // group_m, middle, 0)
    group_b = GROUPS[2]

    def backward(i, carry):
        parts = []
        for j in range(group_b):
            at = pl.ds(i * group_b + j, N, stride=N)
            value = jnp.concatenate([work0[at, :], work1[at, :]], axis=1)
            parts.append(left3(left, value))
        value = jnp.concatenate(parts, axis=0)
        at = rows_of(i, group_b)
        orb[at, :] = right3(value, turn_hi, turn_lo) * orb[at, :]
        return carry

    lax.fori_loop(0, N // group_b, backward, 0)


def leave_grid(leave_ref, orb, field_hi, field_lo):
    leave_hi = leave_ref[0]
    both = jnp.concatenate([leave_hi, leave_ref[1]], axis=0)
    step = 768
    for start in range(0, COLS, step):
        at = slice(start, start + step)
        high, low = split(orb[at, :])
        pieces = dot_nt(both, high)
        field = pieces[0:N] + pieces[N : 2 * N] + dot_nt(leave_hi, low)
        field_hi[:, at], field_lo[:, at] = split(field)


def project(t, w_hi, w_lo, field_hi, field_lo, result):
    cols = slice(2 * t * STK, 2 * (t + 1) * STK)
    high, low = field_hi[...], field_lo[...]
    pieces = dot(jnp.concatenate([high, low], axis=0), w_hi[:, cols])
    total = pieces[0:N] + pieces[N : 2 * N] + dot(high, w_lo[:, cols])
    result[2 * t] = total[:, 0:STK]
    result[2 * t + 1] = total[:, STK : 2 * STK]


def everything(
    coefs_ref, miller_ref, count_ref, left_src, turn_src, enter_src, leave_src, out_ref,
    slots, tables, w_hi, w_lo, orb, work0, work1, kern, cas_y, field_hi, field_lo, result, mine,
    left_ref, turn_ref, enter_ref, leave_ref,
    table_send, table_recv, deal_send, slot_recv, pass_send, back_send, back_recv, local_sem,
):
    owner = lax.axis_index("pw")
    group = lax.axis_index("band")
    groups = lax.axis_size("band")
    side = 1 - 2 * (group % 2)
    partner = (group + side + groups) % groups
    near = (group - side + groups) % groups
    far = (group + 2 * side + groups) % groups
    barrier = pltpu.get_barrier_semaphore()
    for r in range(1, OWNERS):
        pl.semaphore_signal(barrier, inc=1, device_id={"pw": (owner + r) % OWNERS}, device_id_type=MESH)
    for shift in SHIFTS:
        pl.semaphore_signal(barrier, inc=1, device_id={"band": (group + shift + groups) % groups}, device_id_type=MESH)
    keep = pltpu.make_async_copy(coefs_ref.at[0, owner], slots.at[0, 0], local_sem.at[0])
    keep.start()
    loads = []
    for at, (src, dst) in enumerate(
        ((left_src, left_ref), (enter_src, enter_ref), (turn_src, turn_ref), (leave_src, leave_ref))
    ):
        load = pltpu.make_async_copy(src, dst, local_sem.at[at + 1])
        load.start()
        loads.append(load)
    live = jnp.where(lax.broadcasted_iota(I32, (1, STK), 1) < count_ref[0], 1, 0)
    my_table = jnp.concatenate([miller_ref[...], live, jnp.zeros((5, STK), I32)], axis=0)
    mine[...] = my_table
    tables[0] = my_table
    pl.semaphore_wait(barrier, OWNERS - 1 + len(SHIFTS))

    table_sends, deals = [], []
    for r in range(1, OWNERS):
        send = pltpu.make_async_remote_copy(
            src_ref=mine, dst_ref=tables.at[r],
            send_sem=table_send.at[r - 1], recv_sem=table_recv.at[r - 1],
            device_id={"pw": (owner + r) % OWNERS}, device_id_type=MESH)
        send.start()
        table_sends.append(send)
    for r in range(1, OWNERS):
        target = (owner + r) % OWNERS
        send = pltpu.make_async_remote_copy(
            src_ref=coefs_ref.at[0, target], dst_ref=slots.at[0, r],
            send_sem=deal_send.at[r - 1], recv_sem=slot_recv.at[0, r],
            device_id={"pw": target}, device_id_type=MESH)
        send.start()
        deals.append(send)

    passed = {}

    def hand(slot, r, source, target):
        send = pltpu.make_async_remote_copy(
            src_ref=slots.at[source, r], dst_ref=slots.at[slot, r],
            send_sem=pass_send.at[slot - 1, r], recv_sem=slot_recv.at[slot, r],
            device_id={"band": target}, device_id_type=MESH)
        send.start()
        passed[slot, r] = send

    def pass_on(r):
        hand(2, r, 0, near)
        hand(3, r, 0, far)
        hand(1, r, 0, partner)

    keep.wait()
    pass_on(0)
    screened_kernel(kern)
    for r in range(1, OWNERS):
        deals[r - 1].wait_recv()
        pass_on(r)
    for send in table_sends:
        send.wait_recv()
    for load in loads:
        load.wait()
    stick_weights(tables, left_ref, cas_y, w_hi, w_lo)
    for t in range(OWNERS // 2 + 1):
        if t < OWNERS // 2:
            for r in (2 * t, 2 * t + 1):
                passed[2, r].wait_recv()
                hand(4, r, 2, partner)
        if t > 0:
            for slot in (1, 3, 4):
                for r in (2 * t - 2, 2 * t - 1):
                    passed[slot, r].wait_recv()
            synthesize(t - 1, slots, enter_ref, w_hi, w_lo, orb)
    pair_fields(left_ref, turn_ref, orb, work0, work1, kern)
    leave_grid(leave_ref, orb, field_hi, field_lo)

    back = []
    for t in (1, 2, 3, 0):
        project(t, w_hi, w_lo, field_hi, field_lo, result)
        for r in (2 * t, 2 * t + 1):
            if r == 0:
                keep = pltpu.make_async_copy(result.at[0], out_ref.at[0, owner], local_sem.at[0])
                keep.start()
                continue
            source = (owner + OWNERS - r) % OWNERS
            send = pltpu.make_async_remote_copy(
                src_ref=result.at[r], dst_ref=out_ref.at[0, owner],
                send_sem=back_send.at[r - 1], recv_sem=back_recv.at[r - 1],
                device_id={"pw": source}, device_id_type=MESH)
            send.start()
            back.append(send)
    for send in table_sends + deals + list(passed.values()):
        send.wait_send()
    keep.wait()
    for send in back:
        send.wait()


def shards(stick_coefs, miller, stick_count):
    vmem = pl.BlockSpec(memory_space=pltpu.VMEM)
    smem = pl.BlockSpec(memory_space=pltpu.SMEM)
    hbm = pl.BlockSpec(memory_space=pl.ANY)
    dma = pltpu.SemaphoreType.DMA
    consts = [jnp.asarray(t) for t in constant_tables()]
    return pl.pallas_call(
        everything,
        out_shape=jax.ShapeDtypeStruct((1, OWNERS, N, STK), F32),
        in_specs=[hbm, vmem, smem] + [hbm] * 4,
        out_specs=hbm,
        scratch_shapes=[
            pltpu.VMEM((PAIRS, OWNERS, N, STK), F32),
            pltpu.VMEM((OWNERS, 8, STK), I32),
            pltpu.VMEM((COLS, STICKS), BF16),
            pltpu.VMEM((COLS, STICKS), BF16),
            pltpu.VMEM((COLS, WIDE), F32),
            pltpu.VMEM((COLS, 128), F32),
            pltpu.VMEM((COLS, 128), F32),
            pltpu.VMEM((COLS, WIDE), F32),
            pltpu.VMEM((N, STICKS), F32),
            pltpu.VMEM((N, COLS), BF16),
            pltpu.VMEM((N, COLS), BF16),
            pltpu.VMEM((OWNERS, N, STK), F32),
            pltpu.VMEM((8, STK), I32),
        ]
        + [pltpu.VMEM(t.shape, t.dtype) for t in consts]
        + [
            dma((OWNERS - 1,)),
            dma((OWNERS - 1,)),
            dma((OWNERS - 1,)),
            dma((PAIRS, OWNERS)),
            dma((PAIRS - 1, OWNERS)),
            dma((OWNERS - 1,)),
            dma((OWNERS - 1,)),
            dma((5,)),
        ],
        compiler_params=pltpu.CompilerParams(
            vmem_limit_bytes=60 * 1024 * 1024, collective_id=0, has_side_effects=True
        ),
        name="exchange",
    )(stick_coefs, miller, stick_count, *consts)


def solution(mesh):
    return jax.shard_map(
        shards,
        mesh=mesh,
        in_specs=(P("band", None, None, "pw"), P(None, "pw"), P("pw")),
        out_specs=P("band", None, None, "pw"),
        check_vma=False,
    )
```

```python
import math

import jax
import jax.numpy as jnp
import numpy as np
from jax import lax
from jax.experimental import pallas as pl
from jax.experimental.pallas import tpu as pltpu
from jax.sharding import PartitionSpec as P

N = 48
HALF = 2
PAIRS = 2 * HALF + 1
COLS = N * N
WIDE = 256
OWNERS = 8
STK = 128
STICKS = OWNERS * STK
F32, BF16, I32 = jnp.float32, jnp.bfloat16, jnp.int32
MESH = pl.DeviceIdType.MESH
SHIFTS = (-2, -1, 1, 2)


def split_table(values):
    high = np.asarray(values, np.float32).astype(jnp.bfloat16)
    rest = np.asarray(values, np.float64) - high.astype(np.float64)
    low = rest.astype(np.float32).astype(jnp.bfloat16)
    tail = (rest - low.astype(np.float64)).astype(np.float32).astype(jnp.bfloat16)
    return high, low, tail


def constant_tables():
    index = np.arange(N)
    angles = 2.0 * math.pi / N * ((index[:, None] * index[None, :]) % N)
    cas = np.cos(angles) + np.sin(angles)
    high, low, tail = split_table(cas)
    left = np.concatenate([high, high, low], axis=1)
    exact = np.concatenate([high, low, tail], axis=1)
    block = np.kron(np.eye(PAIRS), cas)
    block = np.pad(block, ((0, WIDE - PAIRS * N), (0, WIDE - PAIRS * N)))
    turn = split_table(block)[:2]
    enter = split_table(block * N**-1.5)[:2]
    leave = np.pad(np.tile(-cas * N**-1.5, (1, PAIRS)), ((0, 0), (0, WIDE - PAIRS * N)))
    leave = split_table(leave)[:2]
    return [np.stack([left, exact]), np.stack(turn), np.stack(enter), np.stack(leave)]


def split(value):
    high = value.astype(BF16)
    low = (value - high.astype(F32)).astype(BF16)
    return high, low


def dot(a, b):
    return lax.dot_general(a, b, (((1,), (0,)), ((), ())), preferred_element_type=F32)


def dot_nt(a, b):
    return lax.dot_general(a, b, (((1,), (1,)), ((), ())), preferred_element_type=F32)


def left3(table, value):
    high, low = split(value)
    return dot(table, jnp.concatenate([high, low, high], axis=0))


def right3(value, high_t, low_t):
    high, low = split(value)
    return dot(high, high_t) + dot(low, high_t) + dot(high, low_t)


def rows_of(y, count=1):
    return pl.ds(pl.multiple_of(y * (count * N), count * N), count * N)


def screened_kernel(kern):
    lanes = lax.broadcasted_iota(I32, (1, WIDE), 1)
    kx = lanes - N * (lanes // N)
    kx = jnp.where(kx < N // 2, kx, kx - N)
    rows = lax.broadcasted_iota(I32, (N, 1), 0)
    kz = jnp.where(rows < N // 2, rows, rows - N)
    flat_q = (kz * kz + kx * kx).astype(F32)

    def slab(y, carry):
        signed = jnp.where(y < N // 2, y, y - N)
        q = flat_q + (signed * signed).astype(F32)
        scaled = jnp.maximum(q, 1.0) * (1.0 / 16.0)
        value = (4.0 / N**3) * (1.0 - jnp.exp(-scaled)) / scaled
        kern[rows_of(y), :] = jnp.where(q > 0, value, 4.0 / N**3)
        return carry

    lax.fori_loop(0, N, slab, 0)


def stick_weights(tables, left_ref, cas_y, w_hi, w_lo):
    table = jnp.concatenate([tables[q] for q in range(OWNERS)], axis=1)
    iy, iz, live = table[0:1, :], table[1:2, :], table[2:3, :]
    grid_rows = lax.broadcasted_iota(I32, (N, STICKS), 0)
    pick_y = jnp.where(grid_rows == iy, 1.0, 0.0).astype(BF16)
    pick_z = jnp.where((grid_rows == iz) & (live > 0), 1.0, 0.0).astype(BF16)
    exact = left_ref[1]
    cas_y[...] = dot(exact, jnp.concatenate([pick_y] * 3, axis=0))
    cas_z = dot(exact, jnp.concatenate([pick_z] * 3, axis=0))

    def slab(y, carry):
        high, low = split(cas_y[pl.ds(y, 1), :] * cas_z)
        w_hi[rows_of(y), :] = high
        w_lo[rows_of(y), :] = low
        return carry

    lax.fori_loop(0, N, slab, 0)


def synthesize(t, slots, enter_ref, w_hi, w_lo, orb):
    enter_hi, enter_lo = enter_ref[0, :, 0 : PAIRS * N], enter_ref[1, :, 0 : PAIRS * N]
    coefs = [jnp.concatenate([slots[d, r] for d in range(PAIRS)], axis=0) for r in (2 * t, 2 * t + 1)]
    high, low = split(jnp.concatenate(coefs, axis=1))
    lines = dot(enter_hi, high) + dot(enter_hi, low) + dot(enter_lo, high)
    line_hi, line_lo = split(lines)
    cols = slice(2 * t * STK, 2 * (t + 1) * STK)
    step = 384
    for start in range(0, COLS, step):
        at = slice(start, start + step)
        wh, wl = w_hi[at, cols], w_lo[at, cols]
        part = dot_nt(wh, line_hi) + dot_nt(wh, line_lo) + dot_nt(wl, line_hi)
        orb[at, :] = part if t == 0 else orb[at, :] + part


def spread_own(value):
    own = value[:, 0:128]
    lane = lax.broadcasted_iota(I32, own.shape, 1)
    by96 = pltpu.roll(own, 96, 1)
    first = jnp.where(lane < 48, own, jnp.where(lane < 96, pltpu.roll(own, 48, 1), by96))
    second = jnp.where(lane < 16, by96, jnp.where(lane < 64, pltpu.roll(own, 16, 1), pltpu.roll(own, 64, 1)))
    return jnp.concatenate([first, second], axis=1)


GROUPS = (24, 48, 24)


def pair_fields(left_ref, turn_ref, orb, work0, work1, kern):
    left = left_ref[0]
    turn_hi, turn_lo = turn_ref[0], turn_ref[1]
    group = GROUPS[0]

    def forward(i, carry):
        value = orb[rows_of(i, group), :]
        density = spread_own(value) * value
        along_x = right3(density, turn_hi, turn_lo)
        for j in range(group):
            res = left3(left, along_x[j * N : (j + 1) * N])
            y = i * group + j
            work0[pl.ds(y, N, stride=N), :] = res[:, 0:128]
            work1[pl.ds(y, N, stride=N), :] = res[:, 128:256]
        return carry

    lax.fori_loop(0, N // group, forward, 0)
    group_m = GROUPS[1]

    def middle(i, carry):
        for j in range(group_m):
            at = rows_of(i * group_m + j)
            value = jnp.concatenate([work0[at, :], work1[at, :]], axis=1)
            res = left3(left, value) * kern[at, :]
            res = left3(left, res)
            work0[at, :] = res[:, 0:128]
            work1[at, :] = res[:, 128:256]
        return carry

    lax.fori_loop(0, N // group_m, middle, 0)
    group_b = GROUPS[2]

    def backward(i, carry):
        parts = []
        for j in range(group_b):
            at = pl.ds(i * group_b + j, N, stride=N)
            value = jnp.concatenate([work0[at, :], work1[at, :]], axis=1)
            parts.append(left3(left, value))
        value = jnp.concatenate(parts, axis=0)
        at = rows_of(i, group_b)
        orb[at, :] = right3(value, turn_hi, turn_lo) * orb[at, :]
        return carry

    lax.fori_loop(0, N // group_b, backward, 0)


def leave_grid(leave_ref, orb, field_hi, field_lo):
    leave_hi = leave_ref[0]
    both = jnp.concatenate([leave_hi, leave_ref[1]], axis=0)
    step = 768
    for start in range(0, COLS, step):
        at = slice(start, start + step)
        high, low = split(orb[at, :])
        pieces = dot_nt(both, high)
        field = pieces[0:N] + pieces[N : 2 * N] + dot_nt(leave_hi, low)
        field_hi[:, at], field_lo[:, at] = split(field)


def project(t, w_hi, w_lo, field_hi, field_lo, result):
    cols = slice(2 * t * STK, 2 * (t + 1) * STK)
    high, low = field_hi[...], field_lo[...]
    pieces = dot(jnp.concatenate([high, low], axis=0), w_hi[:, cols])
    total = pieces[0:N] + pieces[N : 2 * N] + dot(high, w_lo[:, cols])
    result[2 * t] = total[:, 0:STK]
    result[2 * t + 1] = total[:, STK : 2 * STK]


def everything(
    coefs_ref, miller_ref, count_ref, left_src, turn_src, enter_src, leave_src, out_ref,
    slots, tables, w_hi, w_lo, orb, work0, work1, kern, cas_y, field_hi, field_lo, result, mine,
    left_ref, turn_ref, enter_ref, leave_ref,
    table_send, table_recv, deal_send, slot_recv, pass_send, back_send, back_recv, local_sem,
):
    owner = lax.axis_index("pw")
    group = lax.axis_index("band")
    groups = lax.axis_size("band")
    side = 1 - 2 * (group % 2)
    partner = (group + side + groups) % groups
    near = (group - side + groups) % groups
    far = (group + 2 * side + groups) % groups
    barrier = pltpu.get_barrier_semaphore()
    for r in range(1, OWNERS):
        pl.semaphore_signal(barrier, inc=1, device_id={"pw": (owner + r) % OWNERS}, device_id_type=MESH)
    for shift in SHIFTS:
        pl.semaphore_signal(barrier, inc=1, device_id={"band": (group + shift + groups) % groups}, device_id_type=MESH)
    keep = pltpu.make_async_copy(coefs_ref.at[0, owner], slots.at[0, 0], local_sem.at[0])
    keep.start()
    loads = []
    for at, (src, dst) in enumerate(
        ((left_src, left_ref), (enter_src, enter_ref), (turn_src, turn_ref), (leave_src, leave_ref))
    ):
        load = pltpu.make_async_copy(src, dst, local_sem.at[at + 1])
        load.start()
        loads.append(load)
    live = jnp.where(lax.broadcasted_iota(I32, (1, STK), 1) < count_ref[0], 1, 0)
    my_table = jnp.concatenate([miller_ref[...], live, jnp.zeros((5, STK), I32)], axis=0)
    mine[...] = my_table
    tables[0] = my_table
    pl.semaphore_wait(barrier, OWNERS - 1 + len(SHIFTS))

    table_sends, deals = [], []
    for r in range(1, OWNERS):
        send = pltpu.make_async_remote_copy(
            src_ref=mine, dst_ref=tables.at[r],
            send_sem=table_send.at[r - 1], recv_sem=table_recv.at[r - 1],
            device_id={"pw": (owner + r) % OWNERS}, device_id_type=MESH)
        send.start()
        table_sends.append(send)
    for r in range(1, OWNERS):
        target = (owner + r) % OWNERS
        send = pltpu.make_async_remote_copy(
            src_ref=coefs_ref.at[0, target], dst_ref=slots.at[0, r],
            send_sem=deal_send.at[r - 1], recv_sem=slot_recv.at[0, r],
            device_id={"pw": target}, device_id_type=MESH)
        send.start()
        deals.append(send)

    passed = {}

    def hand(slot, r, source, target):
        send = pltpu.make_async_remote_copy(
            src_ref=slots.at[source, r], dst_ref=slots.at[slot, r],
            send_sem=pass_send.at[slot - 1, r], recv_sem=slot_recv.at[slot, r],
            device_id={"band": target}, device_id_type=MESH)
        send.start()
        passed[slot, r] = send

    def pass_on(r):
        hand(2, r, 0, near)
        hand(3, r, 0, far)
        hand(1, r, 0, partner)

    keep.wait()
    pass_on(0)
    screened_kernel(kern)
    for r in range(1, OWNERS):
        deals[r - 1].wait_recv()
        pass_on(r)
    for send in table_sends:
        send.wait_recv()
    for load in loads:
        load.wait()
    stick_weights(tables, left_ref, cas_y, w_hi, w_lo)
    for r in range(OWNERS):
        passed[2, r].wait_recv()
        hand(4, r, 2, partner)
    for t in range(OWNERS // 2):
        for slot in (1, 3, 4):
            for r in (2 * t, 2 * t + 1):
                passed[slot, r].wait_recv()
        synthesize(t, slots, enter_ref, w_hi, w_lo, orb)
    pair_fields(left_ref, turn_ref, orb, work0, work1, kern)
    leave_grid(leave_ref, orb, field_hi, field_lo)

    back = []
    for t in (1, 2, 3, 0):
        project(t, w_hi, w_lo, field_hi, field_lo, result)
        for r in (2 * t, 2 * t + 1):
            if r == 0:
                keep = pltpu.make_async_copy(result.at[0], out_ref.at[0, owner], local_sem.at[0])
                keep.start()
                continue
            source = (owner + OWNERS - r) % OWNERS
            send = pltpu.make_async_remote_copy(
                src_ref=result.at[r], dst_ref=out_ref.at[0, owner],
                send_sem=back_send.at[r - 1], recv_sem=back_recv.at[r - 1],
                device_id={"pw": source}, device_id_type=MESH)
            send.start()
            back.append(send)
    for send in table_sends + deals + list(passed.values()):
        send.wait_send()
    keep.wait()
    for send in back:
        send.wait()


def shards(stick_coefs, miller, stick_count):
    vmem = pl.BlockSpec(memory_space=pltpu.VMEM)
    smem = pl.BlockSpec(memory_space=pltpu.SMEM)
    hbm = pl.BlockSpec(memory_space=pl.ANY)
    dma = pltpu.SemaphoreType.DMA
    consts = [jnp.asarray(t) for t in constant_tables()]
    return pl.pallas_call(
        everything,
        out_shape=jax.ShapeDtypeStruct((1, OWNERS, N, STK), F32),
        in_specs=[hbm, vmem, smem] + [hbm] * 4,
        out_specs=hbm,
        scratch_shapes=[
            pltpu.VMEM((PAIRS, OWNERS, N, STK), F32),
            pltpu.VMEM((OWNERS, 8, STK), I32),
            pltpu.VMEM((COLS, STICKS), BF16),
            pltpu.VMEM((COLS, STICKS), BF16),
            pltpu.VMEM((COLS, WIDE), F32),
            pltpu.VMEM((COLS, 128), F32),
            pltpu.VMEM((COLS, 128), F32),
            pltpu.VMEM((COLS, WIDE), F32),
            pltpu.VMEM((N, STICKS), F32),
            pltpu.VMEM((N, COLS), BF16),
            pltpu.VMEM((N, COLS), BF16),
            pltpu.VMEM((OWNERS, N, STK), F32),
            pltpu.VMEM((8, STK), I32),
        ]
        + [pltpu.VMEM(t.shape, t.dtype) for t in consts]
        + [
            dma((OWNERS - 1,)),
            dma((OWNERS - 1,)),
            dma((OWNERS - 1,)),
            dma((PAIRS, OWNERS)),
            dma((PAIRS - 1, OWNERS)),
            dma((OWNERS - 1,)),
            dma((OWNERS - 1,)),
            dma((5,)),
        ],
        compiler_params=pltpu.CompilerParams(
            vmem_limit_bytes=60 * 1024 * 1024, collective_id=0, has_side_effects=True
        ),
        name="exchange",
    )(stick_coefs, miller, stick_count, *consts)


def solution(mesh):
    return jax.shard_map(
        shards,
        mesh=mesh,
        in_specs=(P("band", None, None, "pw"), P(None, "pw"), P("pw")),
        out_specs=P("band", None, None, "pw"),
        check_vma=False,
    )
```
